32 devices in a mesh: replica: 16 (over z, y, x), dom: 2 (over core).
Axes of the slice: x: 2, y: 2, z: 4, core: 2. Of those that a mesh axis runs over, the one named last changes fastest.
Arguments:
- inputs: bfloat16 [2, 384, 8192], P(None, 'replica', 'dom'), may hold values from -6 to 6
- targets: bfloat16 [2, 384, 8192], P(None, 'replica', 'dom'), may hold values from -0.8984375 to 0.8984375
- w_first: float32 [8192, 8192], P('replica', 'dom'), may hold values from -5 to 5
- acc_first: float32 [8192, 8192], P('replica', 'dom'), may hold values from 0.5 to 8
- w_second: float32 [8192, 8192], P('dom', 'replica'), may hold values from -5 to 5
- acc_second: float32 [8192, 8192], P('dom', 'replica'), may hold values from 0.5 to 8
Outputs:
- new_first: float32 [8192, 8192], P('replica', 'dom')
- new_acc_first: float32 [8192, 8192], P('replica', 'dom')
- new_second: float32 [8192, 8192], P('dom', 'replica')
- new_acc_second: float32 [8192, 8192], P('dom', 'replica')
The draws below stay inside these ranges and needn't reach their ends.
All inputs are finite; a program needn't handle non-finite values.
Results may differ from the reference program's by a relative error of at most 0.015.
Values may be sent and summed in bfloat16 or wider, within the bound.
No kernel may reach another device: no remote copies, remote signals or barrier semaphores. Data moves between devices by JAX's collectives and lax.ppermute only.
A program may use at most 192 MiB of HBM per device.

```python
import math
import jax
import jax.numpy as jnp

K = 8192
ROWS = 384
ROUNDS = 2


def steps_of(stream_key, extent, cuts, least, top_value):
    gain = 1.0
    for dim, blocks in cuts:
        heights = jax.random.uniform(jax.random.fold_in(jax.random.fold_in(stream_key, 6), dim), (blocks,), jnp.float32, least / len(cuts), top_value / len(cuts))
        gain = gain * jnp.repeat(jnp.exp(heights), extent[dim] // blocks).reshape((-1,) + (1,) * (len(extent) - 1 - dim))
    return gain


def centred(rng, shape, deviation, limit, cuts=(), dtype=jnp.bfloat16):
    entries = deviation * jax.random.normal(rng, shape, jnp.float32)
    if cuts:
        entries = entries * steps_of(rng, shape, cuts, -0.22, 0.18)
    return jnp.clip(entries, -limit, limit).astype(dtype)


def setup_inputs(seed: int = 0) -> dict:
    keys = jax.random.split(jax.random.key(seed), 7)
    inputs = centred(keys[0], (ROUNDS, ROWS, K), 1.0, 6.0, ((1, 16), (2, 2)))
    targets = jnp.clip(jax.random.uniform(keys[1], (ROUNDS, ROWS, K), jnp.float32, -0.8984375, 0.8984375) * steps_of(keys[1], (ROUNDS, ROWS, K), ((1, 16), (2, 2)), -0.4, 0.0), -0.8984375, 0.8984375).astype(jnp.bfloat16)
    w_first = centred(keys[2], (K, K), 1.0, 5.0, ((0, 16), (1, 2)), jnp.float32)
    acc_first = jnp.clip(jnp.exp(math.log(8.0) - 2.7725887 * jax.random.uniform(keys[3], (K, K), jnp.float32) ** steps_of(keys[3], (K, K), ((0, 16), (1, 2)), -0.2, 0.2)), 0.5, 8.0)
    w_second = centred(keys[4], (K, K), 1.0, 5.0, ((0, 2), (1, 16)), jnp.float32)
    acc_second = jnp.clip(jnp.exp(math.log(8.0) - 2.7725887 * jax.random.uniform(keys[5], (K, K), jnp.float32) ** steps_of(keys[5], (K, K), ((0, 2), (1, 16)), -0.2, 0.2)), 0.5, 8.0)
    return {"inputs": inputs, "targets": targets, "w_first": w_first, "acc_first": acc_first, "w_second": w_second, "acc_second": acc_second}


learn_rate = 0.05
error_weight = 0.25

def reference(inputs, targets, w_first, acc_first, w_second, acc_second):
    unit_scale = 1.0 / math.sqrt(0.4 * K)
    for round_index in range(ROUNDS):
        first_half = w_first.astype(jnp.bfloat16)
        second_half = w_second.astype(jnp.bfloat16)
        round_batch = inputs[round_index]
        first_out = jnp.tanh(jnp.dot(round_batch, first_half.T, preferred_element_type=jnp.float32) * unit_scale)
        first_rows = first_out.astype(jnp.bfloat16)
        second_out = jnp.tanh(jnp.dot(first_rows, second_half.T, preferred_element_type=jnp.float32) * unit_scale)
        goal_rows = targets[round_index].astype(jnp.float32)
        error_half = ((second_out - goal_rows) * error_weight * (1.0 - second_out * second_out)).astype(jnp.bfloat16)
        second_grad = jnp.dot(error_half.T, first_rows, preferred_element_type=jnp.float32)
        back_pre = jnp.dot(error_half, second_half, preferred_element_type=jnp.float32) * unit_scale
        first_error = (back_pre * (1.0 - first_out * first_out)).astype(jnp.bfloat16)
        first_grad = jnp.dot(first_error.T, round_batch, preferred_element_type=jnp.float32)
        acc_first = acc_first + first_grad * first_grad
        w_first = w_first - learn_rate * first_grad / jnp.sqrt(acc_first)
        acc_second = acc_second + second_grad * second_grad
        w_second = w_second - learn_rate * second_grad / jnp.sqrt(acc_second)
    return (w_first, acc_first, w_second, acc_second)
```

```python
import math

import jax
import jax.numpy as jnp
from jax import lax
from jax.sharding import PartitionSpec as P

learn_rate = 0.05
error_weight = 0.25
pieces = 2


def swap(x, axis, offset):
    return lax.ppermute(x, axis, [(i, i ^ offset) for i in range(lax.axis_size(axis))])


def pair_sum(x, axis):
    step = 1
    while step < lax.axis_size(axis):
        x = x + swap(x.astype(jnp.bfloat16), axis, step).astype(jnp.float32)
        step *= 2
    return x


def gather_rows(own, axis):
    line = jnp.concatenate(
        [own] + [swap(own, axis, 4 * k) for k in range(1, lax.axis_size(axis) // 4)], axis=0
    )
    half = own.shape[1] // 2
    far_a, far_b = swap(line, axis, 1), swap(line, axis, 2)
    corner = jnp.concatenate(
        [swap(far_b[:, :half], axis, 1), swap(far_a[:, half:], axis, 2)], axis=1
    )
    return jnp.concatenate([line, far_b, far_a, corner], axis=0)


def scatter_rows(terms, axis):
    wide, narrow = jnp.float32, jnp.bfloat16
    quarter, half = terms.shape[0] // 4, terms.shape[1] // 2
    near, far_b, far_a, corner = [terms[i * quarter : (i + 1) * quarter] for i in range(4)]
    left = swap(corner[:, :half], axis, 1).astype(wide)
    right = swap(corner[:, half:], axis, 2).astype(wide)
    far_b = jnp.concatenate(
        [(far_b[:, :half].astype(wide) + left).astype(narrow), far_b[:, half:]], axis=1
    )
    far_a = jnp.concatenate(
        [far_a[:, :half], (far_a[:, half:].astype(wide) + right).astype(narrow)], axis=1
    )
    line = near.astype(wide) + swap(far_b, axis, 2).astype(wide) + swap(far_a, axis, 1).astype(wide)
    rows = quarter // (lax.axis_size(axis) // 4)
    sent = line.astype(narrow)
    total = line[:rows]
    for k in range(1, lax.axis_size(axis) // 4):
        total = total + swap(sent[k * rows : (k + 1) * rows], axis, 4 * k).astype(wide)
    return total


def columns(x, count):
    width = x.shape[-1] // count
    return [x[..., i * width : (i + 1) * width] for i in range(count)]


def dot(a, b, over):
    return lax.dot_general(a, b, ((over[:1], over[1:]), ((), ())), preferred_element_type=jnp.float32)


def local(inputs, targets, w_first, acc_first, w_second, acc_second):
    full_width = w_first.shape[1] * lax.axis_size("dom")
    unit_scale = 1.0 / math.sqrt(0.4 * full_width)
    narrow = jnp.bfloat16
    rounds = inputs.shape[0]
    batches = [jnp.concatenate([gather_rows(c, "replica") for c in columns(inputs[r], pieces)], axis=1) for r in range(rounds)]
    for r in range(rounds):
        first_half = w_first.astype(narrow)
        second_half = w_second.astype(narrow)
        batch = batches[r]
        first_out = jnp.tanh(pair_sum(dot(batch, first_half, (1, 1)) * unit_scale, "dom"))
        first_rows = first_out.astype(narrow)
        errors = []
        height = second_half.shape[0] // pieces
        for i, goal in enumerate(columns(targets[r], pieces)):
            part = second_half[i * height : (i + 1) * height]
            terms = (dot(first_rows, part, (1, 1)) * unit_scale).astype(narrow)
            second_out = jnp.tanh(scatter_rows(terms, "replica"))
            own = (
                (second_out - goal.astype(jnp.float32))
                * error_weight
                * (1.0 - second_out * second_out)
            ).astype(narrow)
            errors.append(gather_rows(own, "replica"))
        error_half = jnp.concatenate(errors, axis=1)
        back_pre = pair_sum(dot(error_half, second_half, (1, 0)) * unit_scale, "dom")
        first_error = (back_pre * (1.0 - first_out * first_out)).astype(narrow)
        second_grad = dot(error_half, first_rows, (0, 0))
        first_grad = dot(first_error, batch, (0, 0))
        acc_first = acc_first + first_grad * first_grad
        w_first = w_first - learn_rate * first_grad / jnp.sqrt(acc_first)
        acc_second = acc_second + second_grad * second_grad
        w_second = w_second - learn_rate * second_grad / jnp.sqrt(acc_second)
    return (w_first, acc_first, w_second, acc_second)


def solution(mesh):
    placed = (
        P(None, "replica", "dom"),
        P(None, "replica", "dom"),
        P("replica", "dom"),
        P("replica", "dom"),
        P("dom", "replica"),
        P("dom", "replica"),
    )
    return jax.shard_map(
        local,
        mesh=mesh,
        in_specs=placed,
        out_specs=(
            P("replica", "dom"),
            P("replica", "dom"),
            P("dom", "replica"),
            P("dom", "replica"),
        ),
        check_vma=False,
    )
```

```python
import functools
import math

import jax
import jax.numpy as jnp
from jax import lax
from jax.experimental import pallas as pl
from jax.experimental.pallas import tpu as pltpu
from jax.sharding import PartitionSpec as P

learn_rate = 0.05
error_weight = 0.25
pieces = 2


def swap(x, axis, offset):
    return lax.ppermute(x, axis, [(i, i ^ offset) for i in range(lax.axis_size(axis))])


def pair_sum(x, axis):
    step = 1
    while step < lax.axis_size(axis):
        x = x + swap(x.astype(jnp.bfloat16), axis, step).astype(jnp.float32)
        step *= 2
    return x


def gather_line(own, axis):
    far = [swap(own, axis, 4 * k) for k in range(1, lax.axis_size(axis) // 4)]
    return jnp.concatenate([own] + far, axis=0)


def gather_sides(line, axis):
    return line, swap(line, axis, 2), swap(line, axis, 1)


def gather_corner(line, far_b, far_a, axis):
    half = line.shape[1] // 2
    corners = swap(far_b[:, :half], axis, 1), swap(far_a[:, half:], axis, 2)
    rows = line.shape[0]
    whole = jnp.zeros((4 * rows, line.shape[1]), line.dtype)
    for i, part in enumerate((line, far_b, far_a)):
        whole = lax.dynamic_update_slice(whole, part, (i * rows, 0))
    for i, part in enumerate(corners):
        whole = lax.dynamic_update_slice(whole, part, (3 * rows, i * half))
    return whole


def send_corner(terms, axis):
    quarter, half = terms.shape[0] // 4, terms.shape[1] // 2
    blocks = [terms[i * quarter : (i + 1) * quarter] for i in range(4)]
    return blocks[:3], swap(blocks[3][:, :half], axis, 1), swap(blocks[3][:, half:], axis, 2)


def send_sides(blocks, left, right, axis):
    wide, narrow = jnp.float32, jnp.bfloat16
    near, far_b, far_a = blocks
    half = left.shape[1]
    far_b = jnp.concatenate(
        [(far_b[:, :half].astype(wide) + left.astype(wide)).astype(narrow), far_b[:, half:]], axis=1
    )
    far_a = jnp.concatenate(
        [far_a[:, :half], (far_a[:, half:].astype(wide) + right.astype(wide)).astype(narrow)], axis=1
    )
    return near.astype(wide) + swap(far_b, axis, 2).astype(wide) + swap(far_a, axis, 1).astype(wide)


def scatter_line(line, axis):
    wide, narrow = jnp.float32, jnp.bfloat16
    rows = line.shape[0] // (lax.axis_size(axis) // 4)
    sent = line.astype(narrow)
    total = line[:rows]
    for k in range(1, lax.axis_size(axis) // 4):
        total = total + swap(sent[k * rows : (k + 1) * rows], axis, 4 * k).astype(wide)
    return total


def columns(x, count):
    width = x.shape[-1] // count
    return [x[..., i * width : (i + 1) * width] for i in range(count)]


def dot(a, b, over):
    return lax.dot_general(a, b, ((over[:1], over[1:]), ((), ())), preferred_element_type=jnp.float32)


def update_kernel(*refs, count, held, wide):
    w, total = refs[0][...], refs[1][...]
    outs = refs[2 + 2 * count + held :]
    for i in range(count):
        grad = dot(refs[2 + 2 * i][...], refs[3 + 2 * i][...], (0, 0))
        total = total + grad * grad
        w = w - learn_rate * grad * lax.rsqrt(total)
    outs[0][...] = w.astype(outs[0].dtype)
    if wide:
        outs[1][...] = total


def update(w, total, factors, wide, tile, across, first=0, held=()):
    high, long = w.shape
    rows, run = factors[0][0].shape[0], factors[0][1 if across else 0].shape[1]
    tile = min(tile, run)
    first //= tile
    blocks = run // tile
    if across:
        big = pl.BlockSpec((high, tile), lambda i: (0, i + first))
        sides = [pl.BlockSpec((rows, high), lambda i: (0, 0)), pl.BlockSpec((rows, tile), lambda i: (0, i))]
    else:
        big = pl.BlockSpec((tile, long), lambda i: (i + first, 0))
        sides = [pl.BlockSpec((rows, tile), lambda i: (0, i)), pl.BlockSpec((rows, long), lambda i: (0, 0))]
    if wide:
        shapes = [jax.ShapeDtypeStruct(w.shape, jnp.float32)] * 2
        out = big
    else:
        shapes = [jax.ShapeDtypeStruct((high, run) if across else (run, long), jnp.bfloat16)]
        out = pl.BlockSpec(big.block_shape, (lambda i: (0, i)) if across else (lambda i: (i, 0)))
    done = blocks * tile * (high if across else long)
    count = len(factors)
    return pl.pallas_call(
        functools.partial(update_kernel, count=count, held=len(held), wide=wide),
        grid=(blocks,),
        in_specs=[big, big] + sides * count + [pl.BlockSpec(memory_space=pl.ANY)] * len(held),
        out_specs=[out] * len(shapes),
        out_shape=shapes,
        input_output_aliases={2 + 2 * count + i: i for i in range(len(held))},
        cost_estimate=pl.CostEstimate(
            flops=2 * rows * done * count,
            bytes_accessed=done * (16 if wide else 10),
            transcendentals=done * count,
        ),
        compiler_params=pltpu.CompilerParams(vmem_limit_bytes=32 * 1024 * 1024),
    )(w, total, *[f for pair in factors for f in pair], *held)


def local(inputs, targets, w_first, acc_first, w_second, acc_second):
    full_width = w_first.shape[1] * lax.axis_size("dom")
    unit_scale = 1.0 / math.sqrt(0.4 * full_width)
    narrow = jnp.bfloat16
    rounds = inputs.shape[0]
    axis = "replica"
    height = w_second.shape[0] // pieces

    sides = gather_sides(gather_line(inputs[0], axis), axis)
    batch = gather_corner(*sides, axis)
    first_half = w_first.astype(narrow)
    second_parts = [w_second[i * height : (i + 1) * height].astype(narrow) for i in range(pieces)]
    first_factors, second_factors = [], [[] for _ in range(pieces)]
    for r in range(rounds):
        more = r + 1 < rounds
        if more:
            ahead, _ = lax.optimization_barrier((inputs[r + 1], sides[0]))
            ahead = gather_line(ahead, axis)
        first_out = jnp.tanh(pair_sum(dot(batch, first_half, (1, 1)) * unit_scale, "dom"))
        first_rows = first_out.astype(narrow)
        terms = [(dot(first_rows, part, (1, 1)) * unit_scale).astype(narrow) for part in second_parts]
        lines = [send_sides(*send_corner(t, axis), axis) for t in terms]
        if more:
            ahead, lines = lax.optimization_barrier((ahead, lines))
            sides = gather_sides(ahead, axis)
        errors, own = [], None
        for line, goal in zip(lines, columns(targets[r], pieces)):
            if own is not None:
                line, _ = lax.optimization_barrier((line, own))
            second_out = jnp.tanh(scatter_line(line, axis))
            own = (
                (second_out - goal.astype(jnp.float32))
                * error_weight
                * (1.0 - second_out * second_out)
            ).astype(narrow)
            if more and len(errors) == pieces - 1:
                own, sides = lax.optimization_barrier((own, sides))
            errors.append(gather_corner(*gather_sides(gather_line(own, axis), axis), axis))
        back = sum(dot(error, part, (1, 0)) for error, part in zip(errors, second_parts))
        first_error = (pair_sum(back * unit_scale, "dom") * (1.0 - first_out * first_out)).astype(narrow)
        first_factors.append((first_error, batch))
        for factors, error in zip(second_factors, errors):
            factors.append((error, first_rows))
        if more:
            second_parts = [
                update(w_second, acc_second, factors, False, 1024, False, i * height)[0]
                for i, factors in enumerate(second_factors)
            ]
            first_half = update(w_first, acc_first, first_factors, False, 1024, True)[0]
            batch = gather_corner(*sides, axis)
    new_first, new_acc_first = update(w_first, acc_first, first_factors, True, 1024, True)
    held = ()
    for i, factors in enumerate(second_factors):
        held = update(w_second, acc_second, factors, True, 1024, False, i * height, held)
    new_second, new_acc_second = held
    return (new_first, new_acc_first, new_second, new_acc_second)


def solution(mesh):
    placed = (
        P(None, "replica", "dom"),
        P(None, "replica", "dom"),
        P("replica", "dom"),
        P("replica", "dom"),
        P("dom", "replica"),
        P("dom", "replica"),
    )
    return jax.shard_map(
        local,
        mesh=mesh,
        in_specs=placed,
        out_specs=(
            P("replica", "dom"),
            P("replica", "dom"),
            P("dom", "replica"),
            P("dom", "replica"),
        ),
        check_vma=False,
    )
```

```python
import functools
import math

import jax
import jax.numpy as jnp
from jax import lax
from jax.experimental import pallas as pl
from jax.experimental.pallas import tpu as pltpu
from jax.sharding import PartitionSpec as P

learn_rate = 0.05
error_weight = 0.25
pieces = 2


def swap(x, axis, offset):
    return lax.ppermute(x, axis, [(i, i ^ offset) for i in range(lax.axis_size(axis))])


def pair_sum(x, axis):
    step = 1
    while step < lax.axis_size(axis):
        x = x + swap(x.astype(jnp.bfloat16), axis, step).astype(jnp.float32)
        step *= 2
    return x


def gather_line(own, axis):
    far = [swap(own, axis, 4 * k) for k in range(1, lax.axis_size(axis) // 4)]
    return jnp.concatenate([own] + far, axis=0)


def gather_sides(line, axis):
    return line, swap(line, axis, 2), swap(line, axis, 1)


def gather_corner(line, far_b, far_a, axis):
    half = line.shape[1] // 2
    corners = swap(far_b[:, :half], axis, 1), swap(far_a[:, half:], axis, 2)
    rows = line.shape[0]
    whole = jnp.zeros((4 * rows, line.shape[1]), line.dtype)
    for i, part in enumerate((line, far_b, far_a)):
        whole = lax.dynamic_update_slice(whole, part, (i * rows, 0))
    for i, part in enumerate(corners):
        whole = lax.dynamic_update_slice(whole, part, (3 * rows, i * half))
    return whole


def gather_direct(line, axis):
    return jnp.concatenate([line] + [swap(line, axis, step) for step in (2, 1, 3)], axis=0)


def send_corner(terms, axis):
    quarter, half = terms.shape[0] // 4, terms.shape[1] // 2
    blocks = [terms[i * quarter : (i + 1) * quarter] for i in range(4)]
    return blocks[:3], swap(blocks[3][:, :half], axis, 1), swap(blocks[3][:, half:], axis, 2)


def send_sides(blocks, left, right, axis):
    wide, narrow = jnp.float32, jnp.bfloat16
    near, far_b, far_a = blocks
    half = left.shape[1]
    far_b = jnp.concatenate(
        [(far_b[:, :half].astype(wide) + left.astype(wide)).astype(narrow), far_b[:, half:]], axis=1
    )
    far_a = jnp.concatenate(
        [far_a[:, :half], (far_a[:, half:].astype(wide) + right.astype(wide)).astype(narrow)], axis=1
    )
    return near.astype(wide) + swap(far_b, axis, 2).astype(wide) + swap(far_a, axis, 1).astype(wide)


def scatter_line(line, axis):
    wide, narrow = jnp.float32, jnp.bfloat16
    rows = line.shape[0] // (lax.axis_size(axis) // 4)
    sent = line.astype(narrow)
    total = line[:rows]
    for k in range(1, lax.axis_size(axis) // 4):
        total = total + swap(sent[k * rows : (k + 1) * rows], axis, 4 * k).astype(wide)
    return total


def columns(x, count):
    width = x.shape[-1] // count
    return [x[..., i * width : (i + 1) * width] for i in range(count)]


def dot(a, b, over):
    return lax.dot_general(a, b, ((over[:1], over[1:]), ((), ())), preferred_element_type=jnp.float32)


def update_kernel(*refs, count, held, wide):
    w, total = refs[0][...], refs[1][...]
    outs = refs[2 + 2 * count + held :]
    for i in range(count):
        grad = dot(refs[2 + 2 * i][...], refs[3 + 2 * i][...], (0, 0))
        total = total + grad * grad
        w = w - learn_rate * grad * lax.rsqrt(total)
    outs[0][...] = w.astype(outs[0].dtype)
    if wide:
        outs[1][...] = total


def update(w, total, factors, wide, tile, across, first=0, held=()):
    high, long = w.shape
    rows, run = factors[0][0].shape[0], factors[0][1 if across else 0].shape[1]
    tile = min(tile, run)
    first //= tile
    blocks = run // tile
    if across:
        big = pl.BlockSpec((high, tile), lambda i: (0, i + first))
        sides = [pl.BlockSpec((rows, high), lambda i: (0, 0)), pl.BlockSpec((rows, tile), lambda i: (0, i))]
    else:
        big = pl.BlockSpec((tile, long), lambda i: (i + first, 0))
        sides = [pl.BlockSpec((rows, tile), lambda i: (0, i)), pl.BlockSpec((rows, long), lambda i: (0, 0))]
    if wide:
        shapes = [jax.ShapeDtypeStruct(w.shape, jnp.float32)] * 2
        out = big
    else:
        shapes = [jax.ShapeDtypeStruct((high, run) if across else (run, long), jnp.bfloat16)]
        out = pl.BlockSpec(big.block_shape, (lambda i: (0, i)) if across else (lambda i: (i, 0)))
    done = blocks * tile * (high if across else long)
    count = len(factors)
    return pl.pallas_call(
        functools.partial(update_kernel, count=count, held=len(held), wide=wide),
        grid=(blocks,),
        in_specs=[big, big] + sides * count + [pl.BlockSpec(memory_space=pl.ANY)] * len(held),
        out_specs=[out] * len(shapes),
        out_shape=shapes,
        input_output_aliases={2 + 2 * count + i: i for i in range(len(held))},
        cost_estimate=pl.CostEstimate(
            flops=2 * rows * done * count,
            bytes_accessed=done * (16 if wide else 10),
            transcendentals=done * count,
        ),
        compiler_params=pltpu.CompilerParams(vmem_limit_bytes=32 * 1024 * 1024),
    )(w, total, *[f for pair in factors for f in pair], *held)


def local(inputs, targets, w_first, acc_first, w_second, acc_second):
    full_width = w_first.shape[1] * lax.axis_size("dom")
    unit_scale = 1.0 / math.sqrt(0.4 * full_width)
    narrow = jnp.bfloat16
    rounds = inputs.shape[0]
    axis = "replica"
    height = w_second.shape[0] // pieces

    sides = gather_sides(gather_line(inputs[0], axis), axis)
    batch = gather_corner(*sides, axis)
    first_half = w_first.astype(narrow)
    second_parts = [w_second[i * height : (i + 1) * height].astype(narrow) for i in range(pieces)]
    first_factors, second_factors = [], [[] for _ in range(pieces)]
    for r in range(rounds):
        more = r + 1 < rounds
        if more:
            ahead, _ = lax.optimization_barrier((inputs[r + 1], sides[0]))
            ahead = gather_line(ahead, axis)
        first_out = jnp.tanh(pair_sum(dot(batch, first_half, (1, 1)) * unit_scale, "dom"))
        first_rows = first_out.astype(narrow)
        terms = [(dot(first_rows, part, (1, 1)) * unit_scale).astype(narrow) for part in second_parts]
        lines = [send_sides(*send_corner(t, axis), axis) for t in terms]
        if more:
            ahead, lines = lax.optimization_barrier((ahead, lines))
            sides = gather_sides(ahead, axis)
        errors, backs, parts, held = [], [], [], ()
        own, ready = None, None
        for i, (line, goal) in enumerate(zip(lines, columns(targets[r], pieces))):
            if own is not None:
                line, _ = lax.optimization_barrier((line, own))
            second_out = jnp.tanh(scatter_line(line, axis))
            own = (
                (second_out - goal.astype(jnp.float32))
                * error_weight
                * (1.0 - second_out * second_out)
            ).astype(narrow)
            if more and i == pieces - 1:
                own, sides = lax.optimization_barrier((own, sides))
            row = gather_line(own, axis)
            if not more and i < pieces - 1:
                error = gather_direct(row, axis)
            else:
                plane = gather_sides(row, axis)
                if ready is not None:
                    plane, (backs, parts, held) = lax.optimization_barrier((plane, ready))
                error = gather_corner(*plane, axis)
            errors.append(error)
            second_factors[i].append((error, first_rows))
            backs = backs + [dot(error, second_parts[i], (1, 0))]
            if more:
                parts = parts + list(update(w_second, acc_second, second_factors[i], False, 1024, False, i * height))
            else:
                held = tuple(update(w_second, acc_second, second_factors[i], True, 1024, False, i * height, held))
            ready = (backs, parts, held)
        first_error = (pair_sum(sum(backs) * unit_scale, "dom") * (1.0 - first_out * first_out)).astype(narrow)
        first_factors.append((first_error, batch))
        if more:
            second_parts = parts
            first_half = update(w_first, acc_first, first_factors, False, 1024, True)[0]
            batch = gather_corner(*sides, axis)
    new_first, new_acc_first = update(w_first, acc_first, first_factors, True, 1024, True)
    new_second, new_acc_second = held
    return (new_first, new_acc_first, new_second, new_acc_second)


def solution(mesh):
    placed = (
        P(None, "replica", "dom"),
        P(None, "replica", "dom"),
        P("replica", "dom"),
        P("replica", "dom"),
        P("dom", "replica"),
        P("dom", "replica"),
    )
    return jax.shard_map(
        local,
        mesh=mesh,
        in_specs=placed,
        out_specs=(
            P("replica", "dom"),
            P("replica", "dom"),
            P("dom", "replica"),
            P("dom", "replica"),
        ),
        check_vma=False,
    )
```

```python
import functools
import math

import jax
import jax.numpy as jnp
from jax import lax
from jax.experimental import pallas as pl
from jax.experimental.pallas import tpu as pltpu
from jax.sharding import PartitionSpec as P

learn_rate = 0.05
error_weight = 0.25
pieces = 2


def swap(x, axis, offset):
    return lax.ppermute(x, axis, [(i, i ^ offset) for i in range(lax.axis_size(axis))])


def pair_sum(x, axis):
    step = 1
    while step < lax.axis_size(axis):
        x = x + swap(x.astype(jnp.bfloat16), axis, step).astype(jnp.float32)
        step *= 2
    return x


def line_parts(own, axis):
    return [own] + [swap(own, axis, 4 * k) for k in range(1, lax.axis_size(axis) // 4)]


def gather_line(own, axis):
    return jnp.concatenate(line_parts(own, axis), axis=0)


def gather_sides(line, axis):
    return line, swap(line, axis, 2), swap(line, axis, 1)


def gather_corner(line, far_b, far_a, axis, whole=None, start=0):
    half, rows = line.shape[1] // 2, line.shape[0]
    corners = swap(far_b[:, :half], axis, 1), swap(far_a[:, half:], axis, 2)
    if whole is None:
        whole = jnp.zeros((4 * rows, line.shape[1]), line.dtype)
    for i, part in enumerate((line, far_b, far_a)):
        whole = lax.dynamic_update_slice(whole, part, (i * rows, start))
    for i, part in enumerate(corners):
        whole = lax.dynamic_update_slice(whole, part, (3 * rows, start + i * half))
    return whole


def gather_direct(line, axis):
    return jnp.concatenate([line] + [swap(line, axis, step) for step in (2, 1, 3)], axis=0)


def send_corner(terms, axis):
    quarter, half = terms.shape[0] // 4, terms.shape[1] // 2
    blocks = [terms[i * quarter : (i + 1) * quarter] for i in range(4)]
    return blocks[:3], swap(blocks[3][:, :half], axis, 1), swap(blocks[3][:, half:], axis, 2)


def send_sides(blocks, left, right, axis):
    wide, narrow = jnp.float32, jnp.bfloat16
    near, far_b, far_a = blocks
    half = left.shape[1]
    far_b = jnp.concatenate(
        [(far_b[:, :half].astype(wide) + left.astype(wide)).astype(narrow), far_b[:, half:]], axis=1
    )
    far_a = jnp.concatenate(
        [far_a[:, :half], (far_a[:, half:].astype(wide) + right.astype(wide)).astype(narrow)], axis=1
    )
    return near.astype(wide) + swap(far_b, axis, 2).astype(wide) + swap(far_a, axis, 1).astype(wide)


def scatter_line(line, axis):
    wide, narrow = jnp.float32, jnp.bfloat16
    rows = line.shape[0] // (lax.axis_size(axis) // 4)
    sent = line.astype(narrow)
    total = line[:rows]
    for k in range(1, lax.axis_size(axis) // 4):
        total = total + swap(sent[k * rows : (k + 1) * rows], axis, 4 * k).astype(wide)
    return total


def columns(x, count):
    width = x.shape[-1] // count
    return [x[..., i * width : (i + 1) * width] for i in range(count)]


def dot(a, b, over):
    return lax.dot_general(a, b, ((over[:1], over[1:]), ((), ())), preferred_element_type=jnp.float32)


def update_kernel(*refs, count, held, wide):
    w, total = refs[0][...], refs[1][...]
    outs = refs[2 + 2 * count + held :]
    for i in range(count):
        grad = dot(refs[2 + 2 * i][...], refs[3 + 2 * i][...], (0, 0))
        total = total + grad * grad
        w = w - learn_rate * grad * lax.rsqrt(total)
    outs[0][...] = w.astype(outs[0].dtype)
    if wide:
        outs[1][...] = total


def update(w, total, factors, wide, tile, across, first=0, held=()):
    high, long = w.shape
    rows, run = factors[0][0].shape[0], factors[0][1 if across else 0].shape[1]
    tile = min(tile, run)
    first //= tile
    blocks = run // tile
    if across:
        big = pl.BlockSpec((high, tile), lambda i: (0, i + first))
        sides = [pl.BlockSpec((rows, high), lambda i: (0, 0)), pl.BlockSpec((rows, tile), lambda i: (0, i))]
    else:
        big = pl.BlockSpec((tile, long), lambda i: (i + first, 0))
        sides = [pl.BlockSpec((rows, tile), lambda i: (0, i)), pl.BlockSpec((rows, long), lambda i: (0, 0))]
    if wide:
        shapes = [jax.ShapeDtypeStruct(w.shape, jnp.float32)] * 2
        out = big
    else:
        shapes = [jax.ShapeDtypeStruct((high, run) if across else (run, long), jnp.bfloat16)]
        out = pl.BlockSpec(big.block_shape, (lambda i: (0, i)) if across else (lambda i: (i, 0)))
    done = blocks * tile * (high if across else long)
    count = len(factors)
    return pl.pallas_call(
        functools.partial(update_kernel, count=count, held=len(held), wide=wide),
        grid=(blocks,),
        in_specs=[big, big] + sides * count + [pl.BlockSpec(memory_space=pl.ANY)] * len(held),
        out_specs=[out] * len(shapes),
        out_shape=shapes,
        input_output_aliases={2 + 2 * count + i: i for i in range(len(held))},
        cost_estimate=pl.CostEstimate(
            flops=2 * rows * done * count,
            bytes_accessed=done * (16 if wide else 10),
            transcendentals=done * count,
        ),
        compiler_params=pltpu.CompilerParams(vmem_limit_bytes=32 * 1024 * 1024),
    )(w, total, *[f for pair in factors for f in pair], *held)


def local(inputs, targets, w_first, acc_first, w_second, acc_second):
    full_width = w_first.shape[1] * lax.axis_size("dom")
    unit_scale = 1.0 / math.sqrt(0.4 * full_width)
    narrow = jnp.bfloat16
    rounds = inputs.shape[0]
    axis = "replica"
    height = w_second.shape[0] // pieces

    batch, line = None, None
    for i, own in enumerate(columns(inputs[0], pieces)):
        if line is None:
            batch = jnp.zeros((own.shape[0] * lax.axis_size(axis), inputs.shape[2]), narrow)
        else:
            own, line = lax.optimization_barrier((own, line))
        line = gather_line(own, axis)
        sides = gather_sides(line, axis)
        batch = gather_corner(*sides, axis, batch, i * own.shape[1])
    first_half = w_first.astype(narrow)
    second_parts = [w_second[i * height : (i + 1) * height].astype(narrow) for i in range(pieces)]
    first_factors, second_factors = [], [[] for _ in range(pieces)]
    for r in range(rounds):
        more = r + 1 < rounds
        if more:
            ahead, _ = lax.optimization_barrier((inputs[r + 1], sides[0]))
            ahead = gather_line(ahead, axis)
        first_out = jnp.tanh(pair_sum(dot(batch, first_half, (1, 1)) * unit_scale, "dom"))
        first_rows = first_out.astype(narrow)
        terms = [(dot(first_rows, part, (1, 1)) * unit_scale).astype(narrow) for part in second_parts]
        lines = [send_sides(*send_corner(t, axis), axis) for t in terms]
        if more:
            ahead, lines[0] = lax.optimization_barrier((ahead, lines[0]))
            ahead, _ = lax.optimization_barrier((ahead, lines[-1]))
            sides = gather_sides(ahead, axis)
        errors, backs, parts, held = [], [], [], []
        own, waiting = None, None

        def take(i, error):
            errors.append(error)
            second_factors[i].append((error, first_rows))
            backs.append(dot(error, second_parts[i], (1, 0)))
            if more:
                parts.extend(update(w_second, acc_second, second_factors[i], False, 1024, False, i * height))
            else:
                held[:] = update(w_second, acc_second, second_factors[i], True, 1024, False, i * height, held)

        for i, (line, goal) in enumerate(zip(lines, columns(targets[r], pieces))):
            if own is not None:
                line, _ = lax.optimization_barrier((line, own))
            second_out = jnp.tanh(scatter_line(line, axis))
            own = (
                (second_out - goal.astype(jnp.float32))
                * error_weight
                * (1.0 - second_out * second_out)
            ).astype(narrow)
            if more and i == pieces - 1:
                own, sides = lax.optimization_barrier((own, sides))
            along = line_parts(own, axis)
            if waiting is not None:
                waiting, along[0] = lax.optimization_barrier((waiting, along[0]))
                take(0, gather_corner(*waiting, axis))
            row = jnp.concatenate(along, axis=0)
            if not more and i < pieces - 1:
                take(i, gather_direct(row, axis))
                continue
            plane = gather_sides(row, axis)
            if i < pieces - 1:
                waiting = plane
                continue
            plane, (backs, parts, held) = lax.optimization_barrier((plane, (backs, parts, held)))
            take(i, gather_corner(*plane, axis))
        first_error = (pair_sum(sum(backs) * unit_scale, "dom") * (1.0 - first_out * first_out)).astype(narrow)
        first_factors.append((first_error, batch))
        if more:
            second_parts = parts
            first_half = update(w_first, acc_first, first_factors, False, 1024, True)[0]
            sides, _ = lax.optimization_barrier((sides, plane))
            batch = gather_corner(*sides, axis)
    new_first, new_acc_first = update(w_first, acc_first, first_factors, True, 1024, True)
    new_second, new_acc_second = held
    return (new_first, new_acc_first, new_second, new_acc_second)


def solution(mesh):
    placed = (
        P(None, "replica", "dom"),
        P(None, "replica", "dom"),
        P("replica", "dom"),
        P("replica", "dom"),
        P("dom", "replica"),
        P("dom", "replica"),
    )
    return jax.shard_map(
        local,
        mesh=mesh,
        in_specs=placed,
        out_specs=(
            P("replica", "dom"),
            P("replica", "dom"),
            P("dom", "replica"),
            P("dom", "replica"),
        ),
        check_vma=False,
    )
```

```python
import functools
import math

import jax
import jax.numpy as jnp
from jax import lax
from jax.experimental import pallas as pl
from jax.experimental.pallas import tpu as pltpu
from jax.sharding import PartitionSpec as P

learn_rate = 0.05
error_weight = 0.25
pieces = 2


def swap(x, axis, offset):
    return lax.ppermute(x, axis, [(i, i ^ offset) for i in range(lax.axis_size(axis))])


def pair_sum(x, axis):
    step = 1
    while step < lax.axis_size(axis):
        x = x + swap(x.astype(jnp.bfloat16), axis, step).astype(jnp.float32)
        step *= 2
    return x


def line_parts(own, axis):
    return [own] + [swap(own, axis, 4 * k) for k in range(1, lax.axis_size(axis) // 4)]


def gather_line(own, axis):
    return jnp.concatenate(line_parts(own, axis), axis=0)


def gather_sides(line, axis):
    return line, swap(line, axis, 2), swap(line, axis, 1)


def gather_corner(line, far_b, far_a, axis, whole=None, start=0):
    half, rows = line.shape[1] // 2, line.shape[0]
    corners = swap(far_b[:, :half], axis, 1), swap(far_a[:, half:], axis, 2)
    if whole is None:
        whole = jnp.zeros((4 * rows, line.shape[1]), line.dtype)
    for i, part in enumerate((line, far_b, far_a)):
        whole = lax.dynamic_update_slice(whole, part, (i * rows, start))
    for i, part in enumerate(corners):
        whole = lax.dynamic_update_slice(whole, part, (3 * rows, start + i * half))
    return whole


def gather_direct(line, axis):
    return jnp.concatenate([line] + [swap(line, axis, step) for step in (2, 1, 3)], axis=0)


def send_corner(terms, axis):
    quarter, half = terms.shape[0] // 4, terms.shape[1] // 2
    blocks = [terms[i * quarter : (i + 1) * quarter] for i in range(4)]
    return blocks[:3], swap(blocks[3][:, :half], axis, 1), swap(blocks[3][:, half:], axis, 2)


def send_sides(blocks, left, right, axis):
    wide, narrow = jnp.float32, jnp.bfloat16
    near, far_b, far_a = blocks
    half = left.shape[1]
    far_b = jnp.concatenate(
        [(far_b[:, :half].astype(wide) + left.astype(wide)).astype(narrow), far_b[:, half:]], axis=1
    )
    far_a = jnp.concatenate(
        [far_a[:, :half], (far_a[:, half:].astype(wide) + right.astype(wide)).astype(narrow)], axis=1
    )
    return near.astype(wide) + swap(far_b, axis, 2).astype(wide) + swap(far_a, axis, 1).astype(wide)


def scatter_line(line, axis):
    wide, narrow = jnp.float32, jnp.bfloat16
    rows = line.shape[0] // (lax.axis_size(axis) // 4)
    sent = line.astype(narrow)
    total = line[:rows]
    for k in range(1, lax.axis_size(axis) // 4):
        total = total + swap(sent[k * rows : (k + 1) * rows], axis, 4 * k).astype(wide)
    return total


def columns(x, count):
    width = x.shape[-1] // count
    return [x[..., i * width : (i + 1) * width] for i in range(count)]


def dot(a, b, over):
    return lax.dot_general(a, b, ((over[:1], over[1:]), ((), ())), preferred_element_type=jnp.float32)


def update_kernel(*refs, count, held, wide):
    w, total = refs[0][...], refs[1][...]
    outs = refs[2 + 2 * count + held :]
    for i in range(count):
        grad = dot(refs[2 + 2 * i][...], refs[3 + 2 * i][...], (0, 0))
        total = total + grad * grad
        w = w - learn_rate * grad * lax.rsqrt(total)
    outs[0][...] = w.astype(outs[0].dtype)
    if wide:
        outs[1][...] = total


def update(w, total, factors, wide, tile, across, first=0, held=()):
    high, long = w.shape
    rows, run = factors[0][0].shape[0], factors[0][1 if across else 0].shape[1]
    tile = min(tile, run)
    first //= tile
    blocks = run // tile
    if across:
        big = pl.BlockSpec((high, tile), lambda i: (0, i + first))
        sides = [pl.BlockSpec((rows, high), lambda i: (0, 0)), pl.BlockSpec((rows, tile), lambda i: (0, i))]
    else:
        big = pl.BlockSpec((tile, long), lambda i: (i + first, 0))
        sides = [pl.BlockSpec((rows, tile), lambda i: (0, i)), pl.BlockSpec((rows, long), lambda i: (0, 0))]
    if wide:
        shapes = [jax.ShapeDtypeStruct(w.shape, jnp.float32)] * 2
        out = big
    else:
        shapes = [jax.ShapeDtypeStruct((high, run) if across else (run, long), jnp.bfloat16)]
        out = pl.BlockSpec(big.block_shape, (lambda i: (0, i)) if across else (lambda i: (i, 0)))
    done = blocks * tile * (high if across else long)
    count = len(factors)
    return pl.pallas_call(
        functools.partial(update_kernel, count=count, held=len(held), wide=wide),
        grid=(blocks,),
        in_specs=[big, big] + sides * count + [pl.BlockSpec(memory_space=pl.ANY)] * len(held),
        out_specs=[out] * len(shapes),
        out_shape=shapes,
        input_output_aliases={2 + 2 * count + i: i for i in range(len(held))},
        cost_estimate=pl.CostEstimate(
            flops=2 * rows * done * count,
            bytes_accessed=done * (16 if wide else 10),
            transcendentals=done * count,
        ),
        compiler_params=pltpu.CompilerParams(vmem_limit_bytes=32 * 1024 * 1024),
    )(w, total, *[f for pair in factors for f in pair], *held)


def local(inputs, targets, w_first, acc_first, w_second, acc_second):
    full_width = w_first.shape[1] * lax.axis_size("dom")
    unit_scale = 1.0 / math.sqrt(0.4 * full_width)
    narrow = jnp.bfloat16
    rounds = inputs.shape[0]
    axis = "replica"
    height = w_second.shape[0] // pieces

    batch, line = None, None
    for i, own in enumerate(columns(inputs[0], pieces)):
        if line is None:
            batch = jnp.zeros((own.shape[0] * lax.axis_size(axis), inputs.shape[2]), narrow)
        else:
            own, line = lax.optimization_barrier((own, line))
        line = gather_line(own, axis)
        sides = gather_sides(line, axis)
        batch = gather_corner(*sides, axis, batch, i * own.shape[1])
    first_half = w_first.astype(narrow)
    second_parts = [w_second[i * height : (i + 1) * height].astype(narrow) for i in range(pieces)]
    first_factors, second_factors = [], [[] for _ in range(pieces)]
    for r in range(rounds):
        more = r + 1 < rounds
        if more:
            ahead, _ = lax.optimization_barrier((inputs[r + 1], sides[0]))
            ahead = gather_line(ahead, axis)
        first_out = jnp.tanh(pair_sum(dot(batch, first_half, (1, 1)) * unit_scale, "dom"))
        first_rows = first_out.astype(narrow)
        terms = [(dot(first_rows, part, (1, 1)) * unit_scale).astype(narrow) for part in second_parts]
        lines = [send_sides(*send_corner(t, axis), axis) for t in terms]
        if more:
            ahead, lines[0] = lax.optimization_barrier((ahead, lines[0]))
            ahead, _ = lax.optimization_barrier((ahead, lines[-1]))
            sides = gather_sides(ahead, axis)
        errors, backs, parts, held = [], [], [], []
        own, waiting = None, None

        def take(i, error):
            errors.append(error)
            second_factors[i].append((error, first_rows))
            backs.append(dot(error, second_parts[i], (1, 0)))
            if more:
                parts.extend(update(w_second, acc_second, second_factors[i], False, 1024, False, i * height))
            else:
                held[:] = update(w_second, acc_second, second_factors[i], True, 1024, False, i * height, held)

        for i, (line, goal) in enumerate(zip(lines, columns(targets[r], pieces))):
            if own is not None:
                line, _ = lax.optimization_barrier((line, own))
            second_out = jnp.tanh(scatter_line(line, axis))
            own = (
                (second_out - goal.astype(jnp.float32))
                * error_weight
                * (1.0 - second_out * second_out)
            ).astype(narrow)
            along = line_parts(own, axis)
            if waiting is not None:
                waiting, along[0] = lax.optimization_barrier((waiting, along[0]))
                if more:
                    waiting, sides = lax.optimization_barrier((waiting, sides))
                take(0, gather_corner(*waiting, axis))
            row = jnp.concatenate(along, axis=0)
            if not more and i < pieces - 1:
                take(i, gather_direct(row, axis))
                continue
            plane = gather_sides(row, axis)
            if i < pieces - 1:
                waiting = plane
                continue
            plane, (backs, parts, held) = lax.optimization_barrier((plane, (backs, parts, held)))
            take(i, gather_corner(*plane, axis))
        first_error = (pair_sum(sum(backs) * unit_scale, "dom") * (1.0 - first_out * first_out)).astype(narrow)
        first_factors.append((first_error, batch))
        if more:
            second_parts = parts
            first_half = update(w_first, acc_first, first_factors, False, 1024, True)[0]
            sides, _ = lax.optimization_barrier((sides, plane))
            batch = gather_corner(*sides, axis)
    new_first, new_acc_first = update(w_first, acc_first, first_factors, True, 1024, True)
    new_second, new_acc_second = held
    return (new_first, new_acc_first, new_second, new_acc_second)


def solution(mesh):
    placed = (
        P(None, "replica", "dom"),
        P(None, "replica", "dom"),
        P("replica", "dom"),
        P("replica", "dom"),
        P("dom", "replica"),
        P("dom", "replica"),
    )
    return jax.shard_map(
        local,
        mesh=mesh,
        in_specs=placed,
        out_specs=(
            P("replica", "dom"),
            P("replica", "dom"),
            P("dom", "replica"),
            P("dom", "replica"),
        ),
        check_vma=False,
    )
```
